256 devices in a mesh: blk: 16 (over x_lo, y, core), head: 16 (over x_hi, z).
Axes of the slice: x: 4 (x_hi: 2, x_lo: 2; x = x_hi * 2 + x_lo), y: 4, z: 8, core: 2. Of those that a mesh axis runs over, the one named last changes fastest.
Arguments:
- queries: bfloat16 [32768, 2048], P(('blk', 'head')), may hold values from -6 to 6
- key_rows: bfloat16 [32768, 2048], P(('blk', 'head')), may hold values from -6 to 6
- value_rows: bfloat16 [32768, 2048], P(('blk', 'head')), may hold values from -6 to 6
- w_out: bfloat16 [2048, 2048], P('head'), may hold values from -0.125 to 0.125
- first_key: int32 [32768], P('blk'), may hold values from 0 to 32765, as said below
Outputs:
- mixed: bfloat16 [32768, 2048], P(('blk', 'head'))
The draws below stay inside these ranges and needn't reach their ends.
Inputs may be any that keep to these rules, and one draw needn't show every extreme that they name: first_key[i] <= max(i - 1, 0) and first_key[i] >= i - 2048; the last bin of each aligned block of 2048 bins has first_key exactly i - 2048 where that is not negative; the next-to-last bin of the sequence has first_key exactly 32765.
All inputs are finite; a program needn't handle non-finite values.
Results may differ from the reference program's by a relative error of at most 0.0055.
Values may be sent and summed in bfloat16 or wider, within the bound.
No kernel may reach another device: no remote copies, remote signals or barrier semaphores. Data moves between devices by JAX's collectives and lax.ppermute only.
A program may use at most 64 MiB of HBM per device.

```python
from functools import partial
import jax
import jax.numpy as jnp
from jax import lax

HEADS = 32
HEAD_DIM = 64
D = 2048
BLOCK_TOK = 2048
SEQ = 32768
N_BLK = 16


def paired_fields(key):
    base = jax.random.fold_in(key, 11)
    key_query, key_keys = jax.random.split(base, 2)
    shape = (SEQ, HEADS, HEAD_DIM)
    query_field = jnp.clip(jax.random.normal(key_query, shape, jnp.float32), -6.0, 6.0)
    key_field = jnp.clip(jax.random.normal(key_keys, shape, jnp.float32), -6.0, 6.0)
    return (query_field.reshape(SEQ, D), key_field.reshape(SEQ, D))


def draw_queries(key, part):
    return paired_fields(key)[0].astype(jnp.bfloat16)


def draw_key_rows(key, part):
    return paired_fields(key)[1].astype(jnp.bfloat16)


def draw_first_key(key, part):
    base = jax.random.fold_in(key, 5)
    reach = jax.random.randint(base, (SEQ,), 1, BLOCK_TOK + 1, dtype=jnp.int32)
    position = jnp.arange(SEQ, dtype=jnp.int32)
    reach = jnp.where(position % BLOCK_TOK == BLOCK_TOK - 1, BLOCK_TOK, reach)
    reach = jnp.where(position == SEQ - 2, 1, reach)
    return jnp.maximum(position - reach, 0).astype(jnp.int32)


def block_levels(stream_key, dims, shards, low, high):
    factor_of = 1.0
    for axis_at, blocks in shards:
        draws = jax.random.uniform(jax.random.fold_in(jax.random.fold_in(stream_key, 6), axis_at), (blocks,), jnp.float32, low / len(shards), high / len(shards))
        factor_of = factor_of * jnp.repeat(jnp.exp(draws), dims[axis_at] // blocks).reshape((-1,) + (1,) * (len(dims) - 1 - axis_at))
    return factor_of


def centred(key, extent, width, limit, shards=(), kind=jnp.bfloat16):
    result = width * jax.random.normal(key, extent, jnp.float32)
    if shards:
        result = result * block_levels(key, extent, shards, -0.22, 0.18)
    return jnp.clip(result, -limit, limit).astype(kind)


def setup_inputs(seed: int = 0) -> dict:
    keys = jax.random.split(jax.random.key(seed), 6)
    queries = draw_queries(jax.random.fold_in(keys[5], 71), 0)
    key_rows = draw_key_rows(jax.random.fold_in(keys[5], 71), 0)
    value_rows = centred(keys[2], (SEQ, D), 1.0, 6.0, ((0, 256),))
    w_out = centred(keys[3], (D, D), D ** -0.5, 0.125, ((0, 16),))
    first_key = draw_first_key(jax.random.fold_in(keys[5], 71), 0)
    return {"queries": queries, "key_rows": key_rows, "value_rows": value_rows, "w_out": w_out, "first_key": first_key}


def attend(query_tile, key_tile, value_tile, lowest, query_pos, key_pos):
    scores = lax.dot_general(query_tile, key_tile, (((1,), (1,)), ((), ())), preferred_element_type=jnp.float32)
    scores = scores * (HEAD_DIM ** -0.5)
    allowed = (key_pos[None, :] >= lowest[:, None]) & (key_pos[None, :] <= query_pos[:, None])
    scores = jnp.where(allowed, scores, -jnp.inf)
    largest = jnp.max(scores, axis=1, keepdims=True)
    powers = jnp.exp(scores - largest)
    totals = jnp.sum(powers, axis=1, keepdims=True)
    weights = powers.astype(jnp.bfloat16)
    context = jnp.dot(weights, value_tile, preferred_element_type=jnp.float32) / totals
    return context.astype(jnp.bfloat16)


def head_block(queries, key_pad, value_pad, first_key, item):
    block_id = item // HEADS
    head_id = item % HEADS
    start = (block_id * BLOCK_TOK).astype(jnp.int32)
    column = (head_id * HEAD_DIM).astype(jnp.int32)
    query_tile = lax.dynamic_slice(queries, (start, column), (BLOCK_TOK, HEAD_DIM))
    key_tile = lax.dynamic_slice(key_pad, (start, column), (2 * BLOCK_TOK, HEAD_DIM))
    value_tile = lax.dynamic_slice(value_pad, (start, column), (2 * BLOCK_TOK, HEAD_DIM))
    lowest = lax.dynamic_slice_in_dim(first_key, start, BLOCK_TOK)
    query_pos = start + jnp.arange(BLOCK_TOK, dtype=jnp.int32)
    key_pos = start - BLOCK_TOK + jnp.arange(2 * BLOCK_TOK, dtype=jnp.int32)
    return attend(query_tile, key_tile, value_tile, lowest, query_pos, key_pos)


def reference(queries, key_rows, value_rows, w_out, first_key):
    padding = jnp.zeros((BLOCK_TOK, D), key_rows.dtype)
    key_pad = jnp.concatenate([padding, key_rows], axis=0)
    value_pad = jnp.concatenate([padding, value_rows], axis=0)
    items = jnp.arange(N_BLK * HEADS, dtype=jnp.int32)
    tiles = lax.map(partial(head_block, queries, key_pad, value_pad, first_key), items)
    context = tiles.reshape(N_BLK, HEADS, BLOCK_TOK, HEAD_DIM).transpose(0, 2, 1, 3).reshape(SEQ, D)
    return jnp.dot(context, w_out, preferred_element_type=jnp.float32).astype(jnp.bfloat16)
```

```python
import math

import jax
import jax.numpy as jnp
from jax import lax
from jax.experimental import pallas as pl
from jax.experimental.pallas import tpu as pltpu
from jax.sharding import PartitionSpec as P

HEAD_DIM = 64
LANES = 128
TILE = 256


def attend_kernel(low_ref, q_ref, own_ref, prev_ref, o_ref, kbuf, vbuf, s_ref, sem):
    t = pl.program_id(0)
    groups = own_ref.shape[0]

    @pl.when(t == 0)
    def _():
        copies = []
        for j, buf in enumerate((kbuf, vbuf)):
            copies.append(
                pltpu.make_async_copy(prev_ref.at[:, j], buf.at[pl.ds(0, groups)], sem.at[2 * j])
            )
            copies.append(
                pltpu.make_async_copy(
                    own_ref.at[:, 1 + j], buf.at[pl.ds(groups, groups)], sem.at[2 * j + 1]
                )
            )
        for copy in copies:
            copy.start()
        for copy in copies:
            copy.wait()

    rows = q_ref.shape[1]
    per_tile = TILE // rows
    blocks = groups // per_tile + 1
    q = q_ref[...].reshape(TILE, LANES)
    lane = lax.broadcasted_iota(jnp.int32, (TILE, LANES), 1)
    key_lane = lax.broadcasted_iota(jnp.int32, (TILE, TILE), 1)
    key_row = lax.broadcasted_iota(jnp.int32, (TILE, TILE), 0)
    low = jnp.concatenate([low_ref[...]] * (TILE // LANES), axis=1)
    zero = jnp.zeros_like(q)
    factor = math.log2(math.e) * HEAD_DIM ** (-0.5)
    outs = []
    for head in range(2):
        mine = (lane < HEAD_DIM) if head == 0 else (lane >= HEAD_DIM)
        q_head = jnp.where(mine, q, zero)
        largest = None
        for kb in range(blocks):
            keys = kbuf[pl.ds(per_tile * (t + kb), per_tile)].reshape(TILE, LANES)
            s = lax.dot_general(
                q_head, keys, (((1,), (1,)), ((), ())), preferred_element_type=jnp.float32
            )
            allowed = (key_lane + kb * TILE) >= low
            if kb == blocks - 1:
                allowed = allowed & (key_lane <= key_row)
            s = jnp.where(allowed, s, -jnp.inf)
            s_ref[head, kb] = s
            top = jnp.maximum(s[:, :LANES], s[:, LANES:])
            largest = top if largest is None else jnp.maximum(largest, top)
        shift = jnp.max(largest, axis=1, keepdims=True) * factor
        total = None
        acc = None
        for kb in range(blocks):
            values = vbuf[pl.ds(per_tile * (t + kb), per_tile)].reshape(TILE, LANES)
            p = jnp.exp2(s_ref[head, kb] * factor - shift)
            part = p[:, :LANES] + p[:, LANES:]
            total = part if total is None else total + part
            term = jnp.dot(p.astype(jnp.bfloat16), values, preferred_element_type=jnp.float32)
            acc = term if acc is None else acc + term
        outs.append(acc / jnp.sum(total, axis=1, keepdims=True))
    out = jnp.where(lane < HEAD_DIM, outs[0], outs[1])
    o_ref[...] = out.astype(jnp.bfloat16).reshape(o_ref.shape)


def attention(low, own, prev):
    groups, _, rows, _ = own.shape
    per_tile = TILE // rows
    tiles = groups // per_tile
    window = groups * rows + TILE
    return pl.pallas_call(
        attend_kernel,
        grid=(tiles,),
        out_shape=jax.ShapeDtypeStruct((groups, rows, LANES), jnp.bfloat16),
        in_specs=[
            pl.BlockSpec((TILE, LANES), lambda t: (t, 0)),
            pl.BlockSpec((per_tile, None, rows, LANES), lambda t: (t, 0, 0, 0)),
            pl.BlockSpec(memory_space=pl.ANY),
            pl.BlockSpec(memory_space=pl.ANY),
        ],
        out_specs=pl.BlockSpec((per_tile, rows, LANES), lambda t: (t, 0, 0)),
        scratch_shapes=[
            pltpu.VMEM((2 * groups, rows, LANES), jnp.bfloat16),
            pltpu.VMEM((2 * groups, rows, LANES), jnp.bfloat16),
            pltpu.VMEM((2, tiles + 1, TILE, TILE), jnp.float32),
            pltpu.SemaphoreType.DMA((4,)),
        ],
        compiler_params=pltpu.CompilerParams(
            dimension_semantics=("arbitrary",), vmem_limit_bytes=32 << 20
        ),
        cost_estimate=pl.CostEstimate(
            flops=8 * groups * rows * window * LANES,
            bytes_accessed=6 * groups * rows * LANES * 2,
            transcendentals=2 * groups * rows * window,
        ),
        name="attend",
    )(low, own, own, prev)


def project_kernel(ctx_ref, mine_ref, other_ref, o_ref, *, core_axis):
    core = lax.rem(lax.axis_index(core_axis), 2)
    ctx = jnp.concatenate([ctx_ref[i] for i in range(ctx_ref.shape[0])], axis=1)
    for ref, place in ((mine_ref, core), (other_ref, 1 - core)):
        out = jnp.dot(ctx, ref[...], preferred_element_type=jnp.float32)
        o_ref[:, pl.ds(pl.multiple_of(place * LANES, LANES), LANES)] = out.astype(jnp.bfloat16)


def project(ctx, mine, other):
    heads, rows, _ = ctx.shape
    pieces, depth, _ = mine.shape
    width = 2 * pieces * LANES
    piece = pl.BlockSpec((None, depth, LANES), lambda g: (g, 0, 0))
    return pl.pallas_call(
        lambda *refs: project_kernel(*refs, core_axis="blk"),
        grid=(pieces,),
        out_shape=jax.ShapeDtypeStruct((rows, width), jnp.bfloat16),
        in_specs=[pl.BlockSpec((heads, rows, LANES), lambda g: (0, 0, 0)), piece, piece],
        out_specs=pl.BlockSpec((rows, 2 * LANES), lambda g: (0, g)),
        compiler_params=pltpu.CompilerParams(dimension_semantics=("arbitrary",)),
        cost_estimate=pl.CostEstimate(
            flops=2 * rows * depth * width, bytes_accessed=2 * depth * width, transcendentals=0
        ),
        name="project",
    )(ctx, mine, other)


def on_device(queries, key_rows, value_rows, w_out, first_key):
    place = lax.axis_index("blk")
    blks = lax.axis_size("blk")
    heads = lax.axis_size("head")
    rows = queries.shape[0]
    span = heads * rows

    column = lax.dynamic_slice(w_out, (0, place * LANES), (w_out.shape[0], LANES))
    column = lax.all_to_all(
        jnp.broadcast_to(column[None], (heads,) + column.shape), "head", 0, 0, tiled=True
    ).reshape(heads * w_out.shape[0], LANES)
    plane = [list(range(core, blks, 2)) for core in range(2)]
    mine = lax.all_to_all(
        jnp.broadcast_to(column[None], (blks // 2,) + column.shape),
        "blk",
        0,
        0,
        axis_index_groups=plane,
        tiled=True,
    )
    other = lax.ppermute(mine, "blk", [(i, i ^ 1) for i in range(blks)])

    split = lambda x: x.reshape(rows, heads, LANES).transpose(1, 0, 2)
    own = lax.all_to_all(
        jnp.stack([split(x) for x in (queries, key_rows, value_rows)], axis=1),
        "head",
        0,
        0,
        tiled=True,
    )
    prev = lax.ppermute(own[:, 1:], "blk", [(i, i + 1) for i in range(blks - 1)])

    tile_start = (jnp.arange(span, dtype=jnp.int32) // TILE) * TILE
    low = first_key - (place * span - span) - tile_start
    low = jnp.broadcast_to(low[:, None], (span, LANES))
    ctx = attention(low, own, prev)
    ctx = lax.all_to_all(ctx, "head", 0, 0, tiled=True)
    return project(ctx, mine, other)


def solution(mesh):
    placed = (
        P(("blk", "head"), None),
        P(("blk", "head"), None),
        P(("blk", "head"), None),
        P("head", None),
        P("blk"),
    )
    return jax.shard_map(
        on_device, mesh=mesh, in_specs=placed, out_specs=P(("blk", "head"), None), check_vma=False
    )
```

```python
import math

import jax
import jax.numpy as jnp
from jax import lax
from jax.experimental import pallas as pl
from jax.experimental.pallas import tpu as pltpu
from jax.sharding import PartitionSpec as P


HEAD_DIM = 64
LANES = 128
TILE = 256


def attend_kernel(low_ref, q_ref, own_ref, prev_ref, o_ref, kbuf, vbuf, s_ref, sem):
    t = pl.program_id(0)
    groups = own_ref.shape[0]

    @pl.when(t == 0)
    def _():
        copies = []
        for j, buf in enumerate((kbuf, vbuf)):
            copies.append(
                pltpu.make_async_copy(prev_ref.at[:, j], buf.at[pl.ds(0, groups)], sem.at[2 * j])
            )
            copies.append(
                pltpu.make_async_copy(
                    own_ref.at[:, 1 + j], buf.at[pl.ds(groups, groups)], sem.at[2 * j + 1]
                )
            )
        for copy in copies:
            copy.start()
        for copy in copies:
            copy.wait()

    rows = q_ref.shape[1]
    per_tile = TILE // rows
    blocks = groups // per_tile + 1
    q = q_ref[...].reshape(TILE, LANES)
    lane = lax.broadcasted_iota(jnp.int32, (TILE, LANES), 1)
    key_lane = lax.broadcasted_iota(jnp.int32, (TILE, TILE), 1)
    key_row = lax.broadcasted_iota(jnp.int32, (TILE, TILE), 0)
    low = jnp.concatenate([low_ref[...]] * (TILE // LANES), axis=1)
    zero = jnp.zeros_like(q)
    factor = math.log2(math.e) * HEAD_DIM ** (-0.5)
    outs = []
    for head in range(2):
        mine = (lane < HEAD_DIM) if head == 0 else (lane >= HEAD_DIM)
        q_head = jnp.where(mine, q, zero)
        largest = None
        for kb in range(blocks):
            keys = kbuf[pl.ds(per_tile * (t + kb), per_tile)].reshape(TILE, LANES)
            s = lax.dot_general(
                q_head, keys, (((1,), (1,)), ((), ())), preferred_element_type=jnp.float32
            )
            allowed = (key_lane + kb * TILE) >= low
            if kb == blocks - 1:
                allowed = allowed & (key_lane <= key_row)
            s = jnp.where(allowed, s, -jnp.inf)
            s_ref[head, kb] = s
            top = jnp.maximum(s[:, :LANES], s[:, LANES:])
            largest = top if largest is None else jnp.maximum(largest, top)
        shift = jnp.max(largest, axis=1, keepdims=True) * factor
        total = None
        acc = None
        for kb in range(blocks):
            values = vbuf[pl.ds(per_tile * (t + kb), per_tile)].reshape(TILE, LANES)
            p = jnp.exp2(s_ref[head, kb] * factor - shift)
            part = p[:, :LANES] + p[:, LANES:]
            total = part if total is None else total + part
            term = jnp.dot(p.astype(jnp.bfloat16), values, preferred_element_type=jnp.float32)
            acc = term if acc is None else acc + term
        outs.append(acc / jnp.sum(total, axis=1, keepdims=True))
    out = jnp.where(lane < HEAD_DIM, outs[0], outs[1])
    o_ref[...] = out.astype(jnp.bfloat16).reshape(o_ref.shape)


def attention(low, own, prev):
    groups, _, rows, _ = own.shape
    per_tile = TILE // rows
    tiles = groups // per_tile
    window = groups * rows + TILE
    return pl.pallas_call(
        attend_kernel,
        grid=(tiles,),
        out_shape=jax.ShapeDtypeStruct((groups, rows, LANES), jnp.bfloat16),
        in_specs=[
            pl.BlockSpec((TILE, LANES), lambda t: (t, 0)),
            pl.BlockSpec((per_tile, None, rows, LANES), lambda t: (t, 0, 0, 0)),
            pl.BlockSpec(memory_space=pl.ANY),
            pl.BlockSpec(memory_space=pl.ANY),
        ],
        out_specs=pl.BlockSpec((per_tile, rows, LANES), lambda t: (t, 0, 0)),
        scratch_shapes=[
            pltpu.VMEM((2 * groups, rows, LANES), jnp.bfloat16),
            pltpu.VMEM((2 * groups, rows, LANES), jnp.bfloat16),
            pltpu.VMEM((2, tiles + 1, TILE, TILE), jnp.float32),
            pltpu.SemaphoreType.DMA((4,)),
        ],
        compiler_params=pltpu.CompilerParams(
            dimension_semantics=("arbitrary",), vmem_limit_bytes=32 << 20
        ),
        cost_estimate=pl.CostEstimate(
            flops=8 * groups * rows * window * LANES,
            bytes_accessed=6 * groups * rows * LANES * 2,
            transcendentals=2 * groups * rows * window,
        ),
        name="attend",
    )(low, own, own, prev)


def project_kernel(ctx_ref, mine_ref, other_ref, o_ref, *, core_axis):
    core = lax.rem(lax.axis_index(core_axis), 2)
    ctx = jnp.concatenate([ctx_ref[i] for i in range(ctx_ref.shape[0])], axis=1)
    for ref, place in ((mine_ref, core), (other_ref, 1 - core)):
        out = jnp.dot(ctx, ref[...], preferred_element_type=jnp.float32)
        o_ref[:, pl.ds(pl.multiple_of(place * LANES, LANES), LANES)] = out.astype(jnp.bfloat16)


def project(ctx, mine, other):
    heads, rows, _ = ctx.shape
    pieces, depth, _ = mine.shape
    width = 2 * pieces * LANES
    piece = pl.BlockSpec((None, depth, LANES), lambda g: (g, 0, 0))
    return pl.pallas_call(
        lambda *refs: project_kernel(*refs, core_axis="blk"),
        grid=(pieces,),
        out_shape=jax.ShapeDtypeStruct((rows, width), jnp.bfloat16),
        in_specs=[pl.BlockSpec((heads, rows, LANES), lambda g: (0, 0, 0)), piece, piece],
        out_specs=pl.BlockSpec((rows, 2 * LANES), lambda g: (0, g)),
        compiler_params=pltpu.CompilerParams(dimension_semantics=("arbitrary",)),
        cost_estimate=pl.CostEstimate(
            flops=2 * rows * depth * width, bytes_accessed=2 * depth * width, transcendentals=0
        ),
        name="project",
    )(ctx, mine, other)


def layer(queries, key_rows, value_rows, w_out, first_key):
    place = lax.axis_index("blk")
    blks = lax.axis_size("blk")
    heads = lax.axis_size("head")
    rows = queries.shape[0]
    span = heads * rows

    column = lax.dynamic_slice(w_out, (0, place * LANES), (w_out.shape[0], LANES))
    split = lambda x: x.reshape(rows, heads, LANES).transpose(1, 0, 2)
    parts = [split(x) for x in (queries, key_rows, value_rows)]
    parts.append(jnp.broadcast_to(column[None], (heads,) + column.shape))
    own = lax.all_to_all(jnp.stack(parts, axis=1), "head", 0, 0, tiled=True)
    prev = lax.ppermute(own[:, 1:3], "blk", [(i, i + 1) for i in range(blks - 1)])
    column = own[:, 3].reshape(heads * w_out.shape[0], LANES)
    plane = [list(range(core, blks, 2)) for core in range(2)]
    mine = lax.all_to_all(
        jnp.broadcast_to(column[None], (blks // 2,) + column.shape),
        "blk",
        0,
        0,
        axis_index_groups=plane,
        tiled=True,
    )
    other = lax.ppermute(mine, "blk", [(i, i ^ 1) for i in range(blks)])

    tile_start = (jnp.arange(span, dtype=jnp.int32) // TILE) * TILE
    low = first_key - (place * span - span) - tile_start
    low = jnp.broadcast_to(low[:, None], (span, LANES))
    ctx = attention(low, own, prev)
    ctx = lax.all_to_all(ctx, "head", 0, 0, tiled=True)
    return project(ctx, mine, other)


def solution(mesh):
    placed = (
        P(("blk", "head"), None),
        P(("blk", "head"), None),
        P(("blk", "head"), None),
        P("head", None),
        P("blk"),
    )
    return jax.shard_map(
        layer, mesh=mesh, in_specs=placed, out_specs=P(("blk", "head"), None), check_vma=False
    )
```

```python
import functools
import math

import jax
import jax.numpy as jnp
from jax import lax
from jax.experimental import pallas as pl
from jax.experimental.pallas import tpu as pltpu
from jax.sharding import PartitionSpec as P

HEAD_DIM = 64
LANES = 128
TILE = 256


def attend_kernel(low_ref, q_ref, own_ref, prev_ref, o_ref, kbuf, vbuf, s_ref, sem):
    t = pl.program_id(0)
    groups = own_ref.shape[0]

    @pl.when(t == 0)
    def _():
        copies = []
        for j, buf in enumerate((kbuf, vbuf)):
            copies.append(
                pltpu.make_async_copy(prev_ref.at[:, j], buf.at[pl.ds(0, groups)], sem.at[2 * j])
            )
            copies.append(
                pltpu.make_async_copy(
                    own_ref.at[:, j], buf.at[pl.ds(groups, groups)], sem.at[2 * j + 1]
                )
            )
        for copy in copies:
            copy.start()
        for copy in copies:
            copy.wait()

    rows = q_ref.shape[1]
    per_tile = TILE // rows
    blocks = groups // per_tile + 1
    q = q_ref[...].reshape(TILE, LANES)
    lane = lax.broadcasted_iota(jnp.int32, (TILE, LANES), 1)
    key_lane = lax.broadcasted_iota(jnp.int32, (TILE, TILE), 1)
    key_row = lax.broadcasted_iota(jnp.int32, (TILE, TILE), 0)
    low = jnp.concatenate([low_ref[...]] * (TILE // LANES), axis=1)
    zero = jnp.zeros_like(q)
    factor = math.log2(math.e) * HEAD_DIM ** (-0.5)
    outs = []
    for head in range(2):
        mine = (lane < HEAD_DIM) if head == 0 else (lane >= HEAD_DIM)
        q_head = jnp.where(mine, q, zero)
        largest = None
        for kb in range(blocks):
            keys = kbuf[pl.ds(per_tile * (t + kb), per_tile)].reshape(TILE, LANES)
            s = lax.dot_general(
                q_head, keys, (((1,), (1,)), ((), ())), preferred_element_type=jnp.float32
            )
            allowed = (key_lane + kb * TILE) >= low
            if kb == blocks - 1:
                allowed = allowed & (key_lane <= key_row)
            s = jnp.where(allowed, s, -jnp.inf)
            s_ref[head, kb] = s
            top = jnp.maximum(s[:, :LANES], s[:, LANES:])
            largest = top if largest is None else jnp.maximum(largest, top)
        shift = jnp.max(largest, axis=1, keepdims=True) * factor
        total = None
        acc = None
        for kb in range(blocks):
            values = vbuf[pl.ds(per_tile * (t + kb), per_tile)].reshape(TILE, LANES)
            p = jnp.exp2(s_ref[head, kb] * factor - shift)
            part = p[:, :LANES] + p[:, LANES:]
            total = part if total is None else total + part
            term = jnp.dot(p.astype(jnp.bfloat16), values, preferred_element_type=jnp.float32)
            acc = term if acc is None else acc + term
        outs.append(acc / jnp.sum(total, axis=1, keepdims=True))
    out = jnp.where(lane < HEAD_DIM, outs[0], outs[1])
    o_ref[...] = out.astype(jnp.bfloat16).reshape(o_ref.shape)


def attention(low, query, own, prev):
    groups, rows, _ = query.shape
    per_tile = TILE // rows
    tiles = groups // per_tile
    window = groups * rows + TILE
    return pl.pallas_call(
        attend_kernel,
        grid=(tiles,),
        out_shape=jax.ShapeDtypeStruct((groups, rows, LANES), jnp.bfloat16),
        in_specs=[
            pl.BlockSpec((TILE, LANES), lambda t: (t, 0)),
            pl.BlockSpec((per_tile, rows, LANES), lambda t: (t, 0, 0)),
            pl.BlockSpec(memory_space=pl.ANY),
            pl.BlockSpec(memory_space=pl.ANY),
        ],
        out_specs=pl.BlockSpec((per_tile, rows, LANES), lambda t: (t, 0, 0)),
        scratch_shapes=[
            pltpu.VMEM((2 * groups, rows, LANES), jnp.bfloat16),
            pltpu.VMEM((2 * groups, rows, LANES), jnp.bfloat16),
            pltpu.VMEM((2, tiles + 1, TILE, TILE), jnp.float32),
            pltpu.SemaphoreType.DMA((4,)),
        ],
        compiler_params=pltpu.CompilerParams(
            dimension_semantics=("arbitrary",), vmem_limit_bytes=32 << 20
        ),
        cost_estimate=pl.CostEstimate(
            flops=8 * groups * rows * window * LANES,
            bytes_accessed=6 * groups * rows * LANES * 2,
            transcendentals=2 * groups * rows * window,
        ),
        name="attend",
    )(low, query, own, prev)


def project_kernel(ctx_ref, *refs, shifts):
    count = 2 * len(shifts)
    pieces, o_ref, held, sem = refs[:count], refs[count], refs[count + 1], refs[count + 2]
    copies = [pltpu.make_async_copy(pieces[i], held.at[i], sem.at[i]) for i in range(count)]
    for copy in copies:
        copy.start()
    here = lax.axis_index("blk")
    core = lax.rem(here, 2)
    x, y = here // 8, lax.rem(here // 2, 4)
    ctx = jnp.concatenate([ctx_ref[i] for i in range(ctx_ref.shape[0])], axis=1)
    for i, (dx, dy) in enumerate(shifts):
        pair = 4 * lax.rem(x + dx, 2) + lax.rem(y + 4 - dy, 4)
        copies[2 * i].wait()
        copies[2 * i + 1].wait()
        w = jnp.concatenate([held[2 * i], held[2 * i + 1]], axis=1)
        out = jnp.dot(ctx, w, preferred_element_type=jnp.float32).astype(jnp.bfloat16)
        for part, where in ((0, core), (1, 1 - core)):
            at = pl.multiple_of((2 * pair + where) * LANES, LANES)
            o_ref[:, pl.ds(at, LANES)] = out[:, part * LANES : (part + 1) * LANES]


def project(ctx, pieces, shifts):
    _, rows, _ = ctx.shape
    depth = pieces[0].shape[0]
    width = len(pieces) * LANES
    return pl.pallas_call(
        functools.partial(project_kernel, shifts=shifts),
        out_shape=jax.ShapeDtypeStruct((rows, width), jnp.bfloat16),
        in_specs=[pl.BlockSpec(memory_space=pltpu.VMEM)]
        + [pl.BlockSpec(memory_space=pl.ANY)] * len(pieces),
        out_specs=pl.BlockSpec(memory_space=pltpu.VMEM),
        scratch_shapes=[
            pltpu.VMEM((len(pieces), depth, LANES), jnp.bfloat16),
            pltpu.SemaphoreType.DMA((len(pieces),)),
        ],
        compiler_params=pltpu.CompilerParams(vmem_limit_bytes=60 << 20),
        cost_estimate=pl.CostEstimate(
            flops=2 * rows * depth * width, bytes_accessed=2 * depth * width, transcendentals=0
        ),
        name="project",
    )(ctx, *pieces)


def layer(queries, key_rows, value_rows, w_out, first_key):
    place = lax.axis_index("blk")
    blks = lax.axis_size("blk")
    heads = lax.axis_size("head")
    rows = queries.shape[0]
    span = heads * rows
    split = lambda x: x.reshape(rows, heads, LANES).transpose(1, 0, 2)

    column = lax.dynamic_slice(w_out, (0, place * LANES), (w_out.shape[0], LANES))
    kvw = lax.all_to_all(
        jnp.stack(
            [
                split(key_rows),
                split(value_rows),
                jnp.broadcast_to(column[None], (heads,) + column.shape),
            ],
            axis=1,
        ),
        "head",
        0,
        0,
        tiled=True,
    )
    prev = lax.ppermute(kvw[:, :2], "blk", [(i, i + 1) for i in range(blks - 1)])
    query = lax.all_to_all(split(queries), "head", 0, 0, tiled=True)

    mine = kvw[:, 2].reshape(heads * w_out.shape[0], LANES)
    shifts = [(dx, dy) for dy in (0, 1, 3, 2) for dx in (0, 1)]
    pieces = []
    for dx, dy in shifts:
        pairs = []
        for i in range(blks):
            x, y, core = i // 8, (i // 2) % 4, i % 2
            pairs.append((i, (x ^ dx) * 8 + ((y + dy) % 4) * 2 + core))
        piece = mine if dx == dy == 0 else lax.ppermute(mine, "blk", pairs)
        other = lax.ppermute(piece, "blk", [(i, i ^ 1) for i in range(blks)])
        pieces += [piece, other]

    tile_start = (jnp.arange(span, dtype=jnp.int32) // TILE) * TILE
    low = first_key - (place * span - span) - tile_start
    low = jnp.broadcast_to(low[:, None], (span, LANES))
    ctx = attention(low, query, kvw, prev)
    ctx = lax.all_to_all(ctx, "head", 0, 0, tiled=True)
    return project(ctx, pieces, shifts)


def solution(mesh):
    placed = (
        P(("blk", "head"), None),
        P(("blk", "head"), None),
        P(("blk", "head"), None),
        P("head", None),
        P("blk"),
    )
    return jax.shard_map(
        layer, mesh=mesh, in_specs=placed, out_specs=P(("blk", "head"), None), check_vma=False
    )
```

```python
import functools
import math

import jax
import jax.numpy as jnp
from jax import lax
from jax.experimental import pallas as pl
from jax.experimental.pallas import tpu as pltpu
from jax.sharding import PartitionSpec as P


HEAD_DIM = 64
LANES = 128
TILE = 256
FACTOR = math.log2(math.e) * HEAD_DIM ** (-0.5)
DOT = (((1,), (1,)), ((), ()))


def scores(q, low, k_ref, s_ref, kbs, base, diag, largest):
    key_lane = lax.broadcasted_iota(jnp.int32, (TILE, TILE), 1)
    key_row = lax.broadcasted_iota(jnp.int32, (TILE, TILE), 0)
    for u, kb in enumerate(kbs):
        keys = k_ref[2 * kb : 2 * kb + 2].reshape(TILE, LANES)
        s = lax.dot_general(q, keys, DOT, preferred_element_type=jnp.float32)
        allowed = (key_lane + (base + kb * TILE)) >= low
        if kb == diag:
            allowed = allowed & (key_lane <= key_row)
        s = jnp.where(allowed, s, -jnp.inf)
        s_ref[u] = s
        top = jnp.maximum(s[:, :LANES], s[:, LANES:])
        largest = top if largest is None else jnp.maximum(largest, top)
    return jnp.max(largest, axis=1, keepdims=True)

def weigh(v_ref, s_ref, kbs, shift):
    total = acc = None
    for u, kb in enumerate(kbs):
        values = v_ref[2 * kb : 2 * kb + 2].reshape(TILE, LANES)
        p = jnp.exp2(s_ref[u] * FACTOR - shift)
        part = p[:, :LANES] + p[:, LANES:]
        total = part if total is None else total + part
        term = jnp.dot(p.astype(jnp.bfloat16), values, preferred_element_type=jnp.float32)
        acc = term if acc is None else acc + term
    return total, acc

def own_kernel(low0, low1, q0, q1, k_ref, v_ref, acc_o, m_o, l_o, s_ref):
    tiles = k_ref.shape[0] // 2
    lane = lax.broadcasted_iota(jnp.int32, (TILE, LANES), 1)
    for j in range(tiles // 2):
        @pl.when(pl.program_id(0) == j)
        def _():
            for slot, (low, q, tile) in enumerate(((low0, q0, j), (low1, q1, tiles - 1 - j))):
                kbs = range(tile + 1)
                low = jnp.concatenate([low[...]] * 2, axis=1)
                q = q[...].reshape(TILE, LANES)
                accs = []
                for head in range(2):
                    mine = (lane < HEAD_DIM) if head == 0 else (lane >= HEAD_DIM)
                    qh = jnp.where(mine, q, jnp.zeros_like(q))
                    top = scores(qh, low, k_ref, s_ref.at[slot, head], kbs, tiles * TILE, tile, None)
                    l, acc = weigh(v_ref, s_ref.at[slot, head], kbs, top * FACTOR)
                    m_o[slot, head] = jnp.broadcast_to(top, (TILE, LANES))
                    l_o[slot, head] = l
                    accs.append(acc)
                acc_o[slot] = jnp.where(lane < HEAD_DIM, accs[0], accs[1])

def prev_kernel(low0, low1, q0, q1, k_ref, v_ref, acc_i, m_i, l_i, o_ref, s_ref, *, head):
    tiles = k_ref.shape[0] // 2
    lane = lax.broadcasted_iota(jnp.int32, (TILE, LANES), 1)
    mine = (lane < HEAD_DIM) if head == 0 else (lane >= HEAD_DIM)
    half = lax.broadcasted_iota(jnp.int32, (HEAD_DIM, LANES), 1) < HEAD_DIM
    for j in range(tiles // 2):
        @pl.when(pl.program_id(0) == j)
        def _():
            for slot, (low, q, tile) in enumerate(((low0, q0, j), (low1, q1, tiles - 1 - j))):
                kbs = range(tile, tiles)
                low = jnp.concatenate([low[...]] * 2, axis=1)
                q = q[...].reshape(TILE, LANES)
                qh = jnp.where(mine, q, jnp.zeros_like(q))
                own = m_i[slot]
                top = scores(qh, low, k_ref, s_ref.at[slot, 0], kbs, 0, None, own)
                shift = top * FACTOR
                l, acc = weigh(v_ref, s_ref.at[slot, 0], kbs, shift)
                keep = jnp.exp2(own * FACTOR - shift)
                l = l + l_i[slot] * keep
                acc = acc + acc_i[slot] * keep
                out = acc / jnp.sum(l, axis=1, keepdims=True)
                for g in range(2):
                    lo = out[g * LANES : g * LANES + HEAD_DIM]
                    hi = out[g * LANES + HEAD_DIM : (g + 1) * LANES]
                    if head == 0:
                        packed = jnp.where(half, lo, pltpu.roll(hi, HEAD_DIM, 1))
                    else:
                        packed = jnp.where(half, pltpu.roll(lo, HEAD_DIM, 1), hi)
                    o_ref[2 * tile + g] = packed.astype(jnp.bfloat16)

def specs(tiles):
    last = tiles - 1
    return dict(
        low0=pl.BlockSpec((TILE, LANES), lambda j: (j, 0)),
        low1=pl.BlockSpec((TILE, LANES), lambda j: (last - j, 0)),
        q0=pl.BlockSpec((2, None, LANES, LANES), lambda j: (j, 0, 0, 0)),
        q1=pl.BlockSpec((2, None, LANES, LANES), lambda j: (last - j, 0, 0, 0)),
        k=pl.BlockSpec((2 * tiles, None, LANES, LANES), lambda j: (0, 0, 0, 0), pipeline_mode=pl.Buffered(1)),
        v=pl.BlockSpec((2 * tiles, None, LANES, LANES), lambda j: (0, 1, 0, 0), pipeline_mode=pl.Buffered(1)),
    )

def scratch(tiles):
    return [pltpu.VMEM((2, 2, tiles, TILE, TILE), jnp.float32)]

def cost(heads, tiles):
    n = heads * tiles * TILE * (tiles + 1) * TILE // 2
    return pl.CostEstimate(flops=4 * n * LANES, bytes_accessed=6 << 20, transcendentals=n)

def own_part(low, qw, kv):
    tiles = kv.shape[0] // 2
    sp = specs(tiles)
    f = jnp.float32
    return pl.pallas_call(
        own_kernel, grid=(tiles // 2,),
        in_specs=[sp[n] for n in ("low0", "low1", "q0", "q1", "k", "v")],
        out_shape=[jax.ShapeDtypeStruct((tiles, TILE, LANES), f), jax.ShapeDtypeStruct((tiles, 2, TILE, LANES), f), jax.ShapeDtypeStruct((tiles, 2, TILE, LANES), f)],
        out_specs=[pl.BlockSpec((2, TILE, LANES), lambda j: (j, 0, 0)), pl.BlockSpec((2, 2, TILE, LANES), lambda j: (j, 0, 0, 0)), pl.BlockSpec((2, 2, TILE, LANES), lambda j: (j, 0, 0, 0))],
        scratch_shapes=scratch(tiles),
        compiler_params=pltpu.CompilerParams(dimension_semantics=("arbitrary",), vmem_limit_bytes=60 << 20),
        cost_estimate=cost(2, tiles), name="own_part")(low, low, qw, qw, kv, kv)

def prev_part(low, qw, prev, state, head):
    tiles = prev.shape[0] // 2
    sp = specs(tiles)
    acc, m, l = state
    stat = pl.BlockSpec((2, None, TILE, LANES), lambda j: (j, head, 0, 0))
    return pl.pallas_call(
        functools.partial(prev_kernel, head=head), grid=(tiles // 2,),
        in_specs=[sp[n] for n in ("low0", "low1", "q0", "q1", "k", "v")] + [pl.BlockSpec((2, TILE, LANES), lambda j: (j, 0, 0)), stat, stat],
        out_shape=jax.ShapeDtypeStruct((2 * tiles, HEAD_DIM, LANES), jnp.bfloat16),
        out_specs=pl.BlockSpec((2 * tiles, HEAD_DIM, LANES), lambda j: (0, 0, 0)),
        scratch_shapes=scratch(tiles),
        compiler_params=pltpu.CompilerParams(dimension_semantics=("arbitrary",), vmem_limit_bytes=60 << 20),
        cost_estimate=cost(1, tiles))(low, low, qw, qw, prev, prev, acc, m, l)


def project_kernel(a_ref, b_ref, *refs):
    count = len(refs) - 3
    pieces, o_ref, held, sem = refs[:count], refs[count], refs[count + 1], refs[count + 2]
    for i in range(count):
        pltpu.make_async_copy(pieces[i], held.at[i], sem.at[i]).start()
    here = lax.axis_index("blk")
    core = lax.rem(here, 2)
    x, y = here // 8, lax.rem(here // 2, 4)
    half = lax.broadcasted_iota(jnp.int32, (HEAD_DIM, LANES), 1) < HEAD_DIM
    low, high = [], []
    for g in range(a_ref.shape[0]):
        a, b = a_ref[g].astype(jnp.float32), b_ref[g].astype(jnp.float32)
        low.append(jnp.where(half, a, pltpu.roll(b, HEAD_DIM, 1)))
        high.append(jnp.where(half, pltpu.roll(a, HEAD_DIM, 1), b))
    ctx = [jnp.concatenate(part, axis=1).astype(jnp.bfloat16) for part in (low, high)]
    ctx = jnp.concatenate(ctx, axis=0)

    def step(i, carry):
        for k in range(2):
            pltpu.make_async_copy(pieces[k], held.at[2 * i + k], sem.at[2 * i + k]).wait()
        turn = i // 2
        dx, dy = lax.rem(i, 2), turn + lax.rem(turn // 2, 2) * (5 - 2 * turn)
        pair = 4 * lax.rem(x + dx, 2) + lax.rem(y + 4 - dy, 4)
        w = jnp.concatenate([held[2 * i], held[2 * i + 1]], axis=1)
        out = jnp.dot(ctx, w, preferred_element_type=jnp.float32).astype(jnp.bfloat16)
        for part, where in ((0, core), (1, 1 - core)):
            at = pl.multiple_of((2 * pair + where) * LANES, LANES)
            o_ref[:, pl.ds(at, LANES)] = out[:, part * LANES : (part + 1) * LANES]
        return carry

    lax.fori_loop(0, count // 2, step, 0)


def project(a, b, pieces):
    rows = 2 * a.shape[1]
    depth = pieces[0].shape[0]
    width = len(pieces) * LANES
    return pl.pallas_call(
        project_kernel,
        out_shape=jax.ShapeDtypeStruct((rows, width), jnp.bfloat16),
        in_specs=[pl.BlockSpec(memory_space=pltpu.VMEM)] * 2
        + [pl.BlockSpec(memory_space=pl.ANY)] * len(pieces),
        out_specs=pl.BlockSpec(memory_space=pltpu.VMEM),
        scratch_shapes=[
            pltpu.VMEM((len(pieces), depth, LANES), jnp.bfloat16),
            pltpu.SemaphoreType.DMA((len(pieces),)),
        ],
        compiler_params=pltpu.CompilerParams(vmem_limit_bytes=60 << 20),
        cost_estimate=pl.CostEstimate(
            flops=2 * rows * depth * width, bytes_accessed=2 * depth * width, transcendentals=0
        ),
        name="project",
    )(a, b, *pieces)


def layer(queries, key_rows, value_rows, w_out, first_key):
    place = lax.axis_index("blk")
    blks = lax.axis_size("blk")
    heads = lax.axis_size("head")
    rows = queries.shape[0]
    span = heads * rows
    split = lambda x: x.reshape(rows, heads, LANES).transpose(1, 0, 2)

    column = lax.dynamic_slice(w_out, (0, place * LANES), (w_out.shape[0], LANES))
    column = jnp.broadcast_to(column[None], (heads,) + column.shape)
    qw = jnp.stack([split(queries), column], axis=1)
    qw = lax.all_to_all(qw, "head", 0, 0, tiled=True)
    kv = jnp.stack([split(key_rows), split(value_rows)], axis=1)
    kv = lax.all_to_all(kv, "head", 0, 0, tiled=True)
    prev = lax.ppermute(kv, "blk", [(i, i + 1) for i in range(blks - 1)])

    mine = qw[:, 1].reshape(heads * w_out.shape[0], LANES)
    far, _ = lax.optimization_barrier((mine, kv))
    pieces = []
    for dy in (0, 1, 3, 2):
        for dx in (0, 1):
            pairs = []
            for i in range(blks):
                x, y, core = i // 8, (i // 2) % 4, i % 2
                pairs.append((i, (x ^ dx) * 8 + ((y + dy) % 4) * 2 + core))
            if dx == dy == 0:
                piece = mine
            else:
                piece = lax.ppermute(far if dy == 2 else mine, "blk", pairs)
            other = lax.ppermute(piece, "blk", [(i, i ^ 1) for i in range(blks)])
            pieces += [piece, other]

    low = jnp.broadcast_to((first_key - (place * span - span))[:, None], (span, LANES))
    state = own_part(low, qw, kv)
    a = prev_part(low, qw, prev, state, 0)
    a = lax.all_to_all(a, "head", 0, 0, tiled=True)
    b = prev_part(low, qw, prev, state, 1)
    b = lax.all_to_all(b, "head", 0, 0, tiled=True)
    return project(a, b, pieces)


def solution(mesh):
    placed = (
        P(("blk", "head"), None),
        P(("blk", "head"), None),
        P(("blk", "head"), None),
        P("head", None),
        P("blk"),
    )
    return jax.shard_map(layer, mesh=mesh, in_specs=placed, out_specs=P(("blk", "head"), None), check_vma=False)
```

```python
import functools
import math

import jax
import jax.numpy as jnp
from jax import lax
from jax.experimental import pallas as pl
from jax.experimental.pallas import tpu as pltpu
from jax.sharding import PartitionSpec as P


HEAD_DIM = 64
LANES = 128
TILE = 256


def attend_kernel(low_ref, q_ref, own_ref, prev_ref, *refs, first):
    o_ref, kbuf, vbuf, s_ref, sem = refs[-5:]
    t = pl.program_id(0) + first
    groups = own_ref.shape[0]

    @pl.when(pl.program_id(0) == 0)
    def _():
        copies = []
        for j, buf in enumerate((kbuf, vbuf)):
            copies.append(
                pltpu.make_async_copy(prev_ref.at[:, j], buf.at[pl.ds(0, groups)], sem.at[2 * j])
            )
            copies.append(
                pltpu.make_async_copy(
                    own_ref.at[:, j], buf.at[pl.ds(groups, groups)], sem.at[2 * j + 1]
                )
            )
        for copy in copies:
            copy.start()
        for copy in copies:
            copy.wait()

    rows = q_ref.shape[1]
    per_tile = TILE // rows
    blocks = groups // per_tile + 1
    q = q_ref[...].reshape(TILE, LANES)
    lane = lax.broadcasted_iota(jnp.int32, (TILE, LANES), 1)
    key_lane = lax.broadcasted_iota(jnp.int32, (TILE, TILE), 1)
    key_row = lax.broadcasted_iota(jnp.int32, (TILE, TILE), 0)
    low = jnp.concatenate([low_ref[...]] * (TILE // LANES), axis=1)
    zero = jnp.zeros_like(q)
    factor = math.log2(math.e) * HEAD_DIM ** (-0.5)
    outs = []
    for head in range(2):
        mine = (lane < HEAD_DIM) if head == 0 else (lane >= HEAD_DIM)
        q_head = jnp.where(mine, q, zero)
        largest = None
        for kb in range(blocks):
            keys = kbuf[pl.ds(per_tile * (t + kb), per_tile)].reshape(TILE, LANES)
            s = lax.dot_general(
                q_head, keys, (((1,), (1,)), ((), ())), preferred_element_type=jnp.float32
            )
            allowed = (key_lane + kb * TILE) >= low
            if kb == blocks - 1:
                allowed = allowed & (key_lane <= key_row)
            s = jnp.where(allowed, s, -jnp.inf)
            s_ref[head, kb] = s
            top = jnp.maximum(s[:, :LANES], s[:, LANES:])
            largest = top if largest is None else jnp.maximum(largest, top)
        shift = jnp.max(largest, axis=1, keepdims=True) * factor
        total = None
        acc = None
        for kb in range(blocks):
            values = vbuf[pl.ds(per_tile * (t + kb), per_tile)].reshape(TILE, LANES)
            p = jnp.exp2(s_ref[head, kb] * factor - shift)
            part = p[:, :LANES] + p[:, LANES:]
            total = part if total is None else total + part
            term = jnp.dot(p.astype(jnp.bfloat16), values, preferred_element_type=jnp.float32)
            acc = term if acc is None else acc + term
        outs.append(acc / jnp.sum(total, axis=1, keepdims=True))
    out = jnp.where(lane < HEAD_DIM, outs[0], outs[1])
    o_ref[...] = out.astype(jnp.bfloat16).reshape(o_ref.shape)


def attention(low, query, own, prev, first, tiles, done):
    groups, rows, _ = query.shape
    per_tile = TILE // rows
    window = groups * rows + TILE
    past = [] if done is None else [done]
    return pl.pallas_call(
        functools.partial(attend_kernel, first=first),
        grid=(tiles,),
        out_shape=jax.ShapeDtypeStruct((groups, rows, LANES), jnp.bfloat16),
        in_specs=[
            pl.BlockSpec((TILE, LANES), lambda t: (t + first, 0)),
            pl.BlockSpec((per_tile, rows, LANES), lambda t: (t + first, 0, 0)),
            pl.BlockSpec(memory_space=pl.ANY),
            pl.BlockSpec(memory_space=pl.ANY),
        ]
        + [pl.BlockSpec(memory_space=pl.ANY)] * len(past),
        out_specs=pl.BlockSpec((per_tile, rows, LANES), lambda t: (t + first, 0, 0)),
        scratch_shapes=[
            pltpu.VMEM((2 * groups, rows, LANES), jnp.bfloat16),
            pltpu.VMEM((2 * groups, rows, LANES), jnp.bfloat16),
            pltpu.VMEM((2, window // TILE, TILE, TILE), jnp.float32),
            pltpu.SemaphoreType.DMA((4,)),
        ],
        compiler_params=pltpu.CompilerParams(
            dimension_semantics=("arbitrary",), vmem_limit_bytes=32 << 20
        ),
        cost_estimate=pl.CostEstimate(
            flops=8 * tiles * TILE * window * LANES,
            bytes_accessed=6 * groups * rows * LANES * 2,
            transcendentals=2 * tiles * TILE * window,
        ),
        input_output_aliases={4: 0} if past else {},
        name="attend",
    )(low, query, own, prev, *past)


def project_kernel(ctx_ref, *refs, shifts):
    count = 2 * len(shifts)
    pieces, o_ref, held, sem = refs[:count], refs[count], refs[count + 1], refs[count + 2]
    copies = [pltpu.make_async_copy(pieces[i], held.at[i], sem.at[i]) for i in range(count)]
    for copy in copies:
        copy.start()
    here = lax.axis_index("blk")
    core = lax.rem(here, 2)
    x, y = here // 8, lax.rem(here // 2, 4)
    ctx = jnp.concatenate([ctx_ref[i] for i in range(ctx_ref.shape[0])], axis=1)
    for i, (dx, dy) in enumerate(shifts):
        pair = 4 * lax.rem(x + dx, 2) + lax.rem(y + 4 - dy, 4)
        copies[2 * i].wait()
        copies[2 * i + 1].wait()
        w = jnp.concatenate([held[2 * i], held[2 * i + 1]], axis=1)
        out = jnp.dot(ctx, w, preferred_element_type=jnp.float32).astype(jnp.bfloat16)
        for part, where in ((0, core), (1, 1 - core)):
            at = pl.multiple_of((2 * pair + where) * LANES, LANES)
            o_ref[:, pl.ds(at, LANES)] = out[:, part * LANES : (part + 1) * LANES]


def project(ctx, pieces, shifts):
    _, rows, _ = ctx.shape
    depth = pieces[0].shape[0]
    width = len(pieces) * LANES
    return pl.pallas_call(
        functools.partial(project_kernel, shifts=shifts),
        out_shape=jax.ShapeDtypeStruct((rows, width), jnp.bfloat16),
        in_specs=[pl.BlockSpec(memory_space=pltpu.VMEM)]
        + [pl.BlockSpec(memory_space=pl.ANY)] * len(pieces),
        out_specs=pl.BlockSpec(memory_space=pltpu.VMEM),
        scratch_shapes=[
            pltpu.VMEM((len(pieces), depth, LANES), jnp.bfloat16),
            pltpu.SemaphoreType.DMA((len(pieces),)),
        ],
        compiler_params=pltpu.CompilerParams(vmem_limit_bytes=50 << 20),
        cost_estimate=pl.CostEstimate(
            flops=2 * rows * depth * width, bytes_accessed=2 * depth * width, transcendentals=0
        ),
        name="project",
    )(ctx, *pieces)


def layer(queries, key_rows, value_rows, w_out, first_key):
    place = lax.axis_index("blk")
    blks = lax.axis_size("blk")
    heads = lax.axis_size("head")
    rows = queries.shape[0]
    span = heads * rows
    split = lambda x: x.reshape(rows, heads, LANES).transpose(1, 0, 2)

    column = lax.dynamic_slice(w_out, (0, place * LANES), (w_out.shape[0], LANES))
    kvw = lax.all_to_all(
        jnp.stack(
            [
                split(key_rows),
                split(value_rows),
                jnp.broadcast_to(column[None], (heads,) + column.shape),
            ],
            axis=1,
        ),
        "head",
        0,
        0,
        tiled=True,
    )
    prev = lax.ppermute(kvw[:, :2], "blk", [(i, i + 1) for i in range(blks - 1)])
    query = split(queries)
    query = lax.all_to_all(query, "head", 0, 0, tiled=True)

    def shift(x, dx, dy):
        pairs = []
        for i in range(blks):
            x0, y0, core = i // 8, (i // 2) % 4, i % 2
            pairs.append((i, (x0 ^ dx) * 8 + ((y0 + dy) % 4) * 2 + core))
        return lax.ppermute(x, "blk", pairs)

    found = {(0, 0): kvw[:, 2].reshape(heads * w_out.shape[0], LANES)}
    for dx, dy in ((0, 1), (1, 3), (1, 1), (0, 3), (1, 0)):
        found[dx, dy] = shift(found[0, 0], dx, dy)
    for dx, dy in ((0, 1), (1, 3)):
        found[dx, 2] = shift(found[dx, dy], 0, dy)
    shifts = [(dx, dy) for dy in (0, 1, 3, 2) for dx in (0, 1)]
    pieces = []
    for at in shifts:
        other = lax.ppermute(found[at], "blk", [(i, i ^ 1) for i in range(blks)])
        pieces += [found[at], other]

    tile_start = (jnp.arange(span, dtype=jnp.int32) // TILE) * TILE
    low = first_key - (place * span - span) - tile_start
    low = jnp.broadcast_to(low[:, None], (span, LANES))
    tiles = span // TILE
    ctx = attention(low, query, kvw, prev, 0, tiles // 2, None)
    ctx = attention(low, query, kvw, prev, tiles // 2, tiles - tiles // 2, ctx)
    ctx = lax.all_to_all(ctx, "head", 0, 0, tiled=True)
    return project(ctx, pieces, shifts)


def solution(mesh):
    placed = (
        P(("blk", "head"), None),
        P(("blk", "head"), None),
        P(("blk", "head"), None),
        P("head", None),
        P("blk"),
    )
    return jax.shard_map(
        layer, mesh=mesh, in_specs=placed, out_specs=P(("blk", "head"), None), check_vma=False
    )
```

```python
import functools
import math

import jax
import jax.numpy as jnp
from jax import lax
from jax.experimental import pallas as pl
from jax.experimental.pallas import tpu as pltpu
from jax.sharding import PartitionSpec as P


HEAD_DIM = 64
LANES = 128
TILE = 256


def attend_kernel(low_ref, q_ref, own_ref, prev_ref, o_ref, kbuf, vbuf, s_ref, sem):
    t = pl.program_id(0)
    groups = own_ref.shape[0]

    @pl.when(t == 0)
    def _():
        copies = []
        for j, buf in enumerate((kbuf, vbuf)):
            copies.append(
                pltpu.make_async_copy(prev_ref.at[:, j], buf.at[pl.ds(0, groups)], sem.at[2 * j])
            )
            copies.append(
                pltpu.make_async_copy(
                    own_ref.at[:, j], buf.at[pl.ds(groups, groups)], sem.at[2 * j + 1]
                )
            )
        for copy in copies:
            copy.start()
        for copy in copies:
            copy.wait()

    rows = q_ref.shape[1]
    per_tile = TILE // rows
    blocks = groups // per_tile + 1
    q = q_ref[...].reshape(TILE, LANES)
    lane = lax.broadcasted_iota(jnp.int32, (TILE, LANES), 1)
    key_lane = lax.broadcasted_iota(jnp.int32, (TILE, TILE), 1)
    key_row = lax.broadcasted_iota(jnp.int32, (TILE, TILE), 0)
    low = jnp.concatenate([low_ref[...]] * (TILE // LANES), axis=1)
    zero = jnp.zeros_like(q)
    factor = math.log2(math.e) * HEAD_DIM ** (-0.5)
    outs = []
    for head in range(2):
        mine = (lane < HEAD_DIM) if head == 0 else (lane >= HEAD_DIM)
        q_head = jnp.where(mine, q, zero)
        largest = None
        for kb in range(blocks):
            keys = kbuf[pl.ds(per_tile * (t + kb), per_tile)].reshape(TILE, LANES)
            s = lax.dot_general(
                q_head, keys, (((1,), (1,)), ((), ())), preferred_element_type=jnp.float32
            )
            allowed = (key_lane + kb * TILE) >= low
            if kb == blocks - 1:
                allowed = allowed & (key_lane <= key_row)
            s = jnp.where(allowed, s, -jnp.inf)
            s_ref[head, kb] = s
            top = jnp.maximum(s[:, :LANES], s[:, LANES:])
            largest = top if largest is None else jnp.maximum(largest, top)
        shift = jnp.max(largest, axis=1, keepdims=True) * factor
        total = None
        acc = None
        for kb in range(blocks):
            values = vbuf[pl.ds(per_tile * (t + kb), per_tile)].reshape(TILE, LANES)
            p = jnp.exp2(s_ref[head, kb] * factor - shift)
            part = p[:, :LANES] + p[:, LANES:]
            total = part if total is None else total + part
            term = jnp.dot(p.astype(jnp.bfloat16), values, preferred_element_type=jnp.float32)
            acc = term if acc is None else acc + term
        outs.append(acc / jnp.sum(total, axis=1, keepdims=True))
    out = jnp.where(lane < HEAD_DIM, outs[0], outs[1])
    o_ref[...] = out.astype(jnp.bfloat16).reshape(o_ref.shape)


def attention(low, query, own, prev):
    groups, rows, _ = query.shape
    per_tile = TILE // rows
    tiles = groups // per_tile
    window = groups * rows + TILE
    return pl.pallas_call(
        attend_kernel,
        grid=(tiles,),
        out_shape=jax.ShapeDtypeStruct((groups, rows, LANES), jnp.bfloat16),
        in_specs=[
            pl.BlockSpec((TILE, LANES), lambda t: (t, 0)),
            pl.BlockSpec((per_tile, rows, LANES), lambda t: (t, 0, 0)),
            pl.BlockSpec(memory_space=pl.ANY),
            pl.BlockSpec(memory_space=pl.ANY),
        ],
        out_specs=pl.BlockSpec((per_tile, rows, LANES), lambda t: (t, 0, 0)),
        scratch_shapes=[
            pltpu.VMEM((2 * groups, rows, LANES), jnp.bfloat16),
            pltpu.VMEM((2 * groups, rows, LANES), jnp.bfloat16),
            pltpu.VMEM((2, tiles + 1, TILE, TILE), jnp.float32),
            pltpu.SemaphoreType.DMA((4,)),
        ],
        compiler_params=pltpu.CompilerParams(
            dimension_semantics=("arbitrary",), vmem_limit_bytes=32 << 20
        ),
        cost_estimate=pl.CostEstimate(
            flops=8 * groups * rows * window * LANES,
            bytes_accessed=6 * groups * rows * LANES * 2,
            transcendentals=2 * groups * rows * window,
        ),
        name="attend",
    )(low, query, own, prev)


def project_kernel(ctx_ref, *refs, shifts):
    count = 2 * len(shifts)
    pieces, o_ref, held, sem = refs[:count], refs[count], refs[count + 1], refs[count + 2]
    copies = [pltpu.make_async_copy(pieces[i], held.at[i], sem.at[i]) for i in range(count)]
    for copy in copies:
        copy.start()
    here = lax.axis_index("blk")
    core = lax.rem(here, 2)
    x, y = here // 8, lax.rem(here // 2, 4)
    ctx = jnp.concatenate([ctx_ref[i] for i in range(ctx_ref.shape[0])], axis=1)
    for i, (dx, dy) in enumerate(shifts):
        pair = 4 * lax.rem(x + dx, 2) + lax.rem(y + 4 - dy, 4)
        copies[2 * i].wait()
        copies[2 * i + 1].wait()
        w = jnp.concatenate([held[2 * i], held[2 * i + 1]], axis=1)
        out = jnp.dot(ctx, w, preferred_element_type=jnp.float32).astype(jnp.bfloat16)
        for part, where in ((0, core), (1, 1 - core)):
            at = pl.multiple_of((2 * pair + where) * LANES, LANES)
            o_ref[:, pl.ds(at, LANES)] = out[:, part * LANES : (part + 1) * LANES]


def project(ctx, pieces, shifts):
    _, rows, _ = ctx.shape
    depth = pieces[0].shape[0]
    width = len(pieces) * LANES
    return pl.pallas_call(
        functools.partial(project_kernel, shifts=shifts),
        out_shape=jax.ShapeDtypeStruct((rows, width), jnp.bfloat16),
        in_specs=[pl.BlockSpec(memory_space=pltpu.VMEM)]
        + [pl.BlockSpec(memory_space=pl.ANY)] * len(pieces),
        out_specs=pl.BlockSpec(memory_space=pltpu.VMEM),
        scratch_shapes=[
            pltpu.VMEM((len(pieces), depth, LANES), jnp.bfloat16),
            pltpu.SemaphoreType.DMA((len(pieces),)),
        ],
        compiler_params=pltpu.CompilerParams(vmem_limit_bytes=50 << 20),
        cost_estimate=pl.CostEstimate(
            flops=2 * rows * depth * width, bytes_accessed=2 * depth * width, transcendentals=0
        ),
        name="project",
    )(ctx, *pieces)


def layer(queries, key_rows, value_rows, w_out, first_key):
    place = lax.axis_index("blk")
    blks = lax.axis_size("blk")
    heads = lax.axis_size("head")
    rows = queries.shape[0]
    span = heads * rows
    split = lambda x: x.reshape(rows, heads, LANES).transpose(1, 0, 2)

    column = lax.dynamic_slice(w_out, (0, place * LANES), (w_out.shape[0], LANES))
    kvw = lax.all_to_all(
        jnp.stack(
            [
                split(key_rows),
                split(value_rows),
                jnp.broadcast_to(column[None], (heads,) + column.shape),
            ],
            axis=1,
        ),
        "head",
        0,
        0,
        tiled=True,
    )
    prev = lax.ppermute(kvw[:, :2], "blk", [(i, i + 1) for i in range(blks - 1)])
    query = split(queries)
    query = lax.all_to_all(query, "head", 0, 0, tiled=True)

    def shift(x, dx, dy):
        pairs = []
        for i in range(blks):
            x0, y0, core = i // 8, (i // 2) % 4, i % 2
            pairs.append((i, (x0 ^ dx) * 8 + ((y0 + dy) % 4) * 2 + core))
        return lax.ppermute(x, "blk", pairs)

    found = {(0, 0): kvw[:, 2].reshape(heads * w_out.shape[0], LANES)}
    for dx, dy in ((0, 1), (1, 3), (1, 1), (0, 3), (1, 0)):
        found[dx, dy] = shift(found[0, 0], dx, dy)
    for dx, dy in ((0, 1), (1, 3)):
        found[dx, 2] = shift(found[dx, dy], 0, dy)
    shifts = [(dx, dy) for dy in (0, 1, 3, 2) for dx in (0, 1)]
    pieces = []
    for at in shifts:
        other = lax.ppermute(found[at], "blk", [(i, i ^ 1) for i in range(blks)])
        pieces += [found[at], other]

    tile_start = (jnp.arange(span, dtype=jnp.int32) // TILE) * TILE
    low = first_key - (place * span - span) - tile_start
    low = jnp.broadcast_to(low[:, None], (span, LANES))
    ctx = attention(low, query, kvw, prev)
    ctx = lax.all_to_all(ctx, "head", 0, 0, tiled=True)
    return project(ctx, pieces, shifts)


def solution(mesh):
    placed = (
        P(("blk", "head"), None),
        P(("blk", "head"), None),
        P(("blk", "head"), None),
        P("head", None),
        P("blk"),
    )
    return jax.shard_map(
        layer, mesh=mesh, in_specs=placed, out_specs=P(("blk", "head"), None), check_vma=False
    )
```

```python
import functools
import math

import jax
import jax.numpy as jnp
from jax import lax
from jax.experimental import pallas as pl
from jax.experimental.pallas import tpu as pltpu
from jax.sharding import PartitionSpec as P


HEAD_DIM = 64
LANES = 128
TILE = 256


def attend_kernel(low_ref, q_ref, own_ref, prev_ref, o_ref, kbuf, vbuf, s_ref, sem):
    t = pl.program_id(0)
    groups = own_ref.shape[0]

    @pl.when(t == 0)
    def _():
        copies = []
        for j, buf in enumerate((kbuf, vbuf)):
            copies.append(
                pltpu.make_async_copy(prev_ref.at[:, j], buf.at[pl.ds(0, groups)], sem.at[2 * j])
            )
            copies.append(
                pltpu.make_async_copy(
                    own_ref.at[:, j], buf.at[pl.ds(groups, groups)], sem.at[2 * j + 1]
                )
            )
        for copy in copies:
            copy.start()
        for copy in copies:
            copy.wait()

    rows = q_ref.shape[1]
    per_tile = TILE // rows
    blocks = groups // per_tile + 1
    q = q_ref[...].reshape(TILE, LANES)
    lane = lax.broadcasted_iota(jnp.int32, (TILE, LANES), 1)
    key_lane = lax.broadcasted_iota(jnp.int32, (TILE, TILE), 1)
    key_row = lax.broadcasted_iota(jnp.int32, (TILE, TILE), 0)
    low = jnp.concatenate([low_ref[...]] * (TILE // LANES), axis=1)
    zero = jnp.zeros_like(q)
    factor = math.log2(math.e) * HEAD_DIM ** (-0.5)
    outs = []
    for head in range(2):
        mine = (lane < HEAD_DIM) if head == 0 else (lane >= HEAD_DIM)
        q_head = jnp.where(mine, q, zero)
        largest = None
        for kb in range(blocks):
            keys = kbuf[pl.ds(per_tile * (t + kb), per_tile)].reshape(TILE, LANES)
            s = lax.dot_general(
                q_head, keys, (((1,), (1,)), ((), ())), preferred_element_type=jnp.float32
            )
            allowed = (key_lane + kb * TILE) >= low
            if kb == blocks - 1:
                allowed = allowed & (key_lane <= key_row)
            s = jnp.where(allowed, s, -jnp.inf)
            s_ref[head, kb] = s
            top = jnp.maximum(s[:, :LANES], s[:, LANES:])
            largest = top if largest is None else jnp.maximum(largest, top)
        shift = jnp.max(largest, axis=1, keepdims=True) * factor
        acc = None
        for kb in range(blocks):
            values = vbuf[pl.ds(per_tile * (t + kb), per_tile)].reshape(TILE, LANES)
            p = jnp.exp2(s_ref[head, kb] * factor - shift)
            values = jnp.where(mine, values, jnp.ones_like(values))
            term = jnp.dot(p.astype(jnp.bfloat16), values, preferred_element_type=jnp.float32)
            acc = term if acc is None else acc + term
        outs.append(acc)
    total = pltpu.roll(jnp.where(lane < HEAD_DIM, outs[1], outs[0]), HEAD_DIM, 1)
    out = jnp.where(lane < HEAD_DIM, outs[0], outs[1]) / total
    o_ref[...] = out.astype(jnp.bfloat16).reshape(o_ref.shape)


def attention(low, query, own, prev):
    groups, rows, _ = query.shape
    per_tile = TILE // rows
    tiles = groups // per_tile
    window = groups * rows + TILE
    return pl.pallas_call(
        attend_kernel,
        grid=(tiles,),
        out_shape=jax.ShapeDtypeStruct((groups, rows, LANES), jnp.bfloat16),
        in_specs=[
            pl.BlockSpec((TILE, LANES), lambda t: (t, 0)),
            pl.BlockSpec((per_tile, rows, LANES), lambda t: (t, 0, 0)),
            pl.BlockSpec(memory_space=pl.ANY),
            pl.BlockSpec(memory_space=pl.ANY),
        ],
        out_specs=pl.BlockSpec((per_tile, rows, LANES), lambda t: (t, 0, 0)),
        scratch_shapes=[
            pltpu.VMEM((2 * groups, rows, LANES), jnp.bfloat16),
            pltpu.VMEM((2 * groups, rows, LANES), jnp.bfloat16),
            pltpu.VMEM((2, tiles + 1, TILE, TILE), jnp.float32),
            pltpu.SemaphoreType.DMA((4,)),
        ],
        compiler_params=pltpu.CompilerParams(
            dimension_semantics=("arbitrary",), vmem_limit_bytes=32 << 20
        ),
        cost_estimate=pl.CostEstimate(
            flops=8 * groups * rows * window * LANES,
            bytes_accessed=6 * groups * rows * LANES * 2,
            transcendentals=2 * groups * rows * window,
        ),
        name="attend",
    )(low, query, own, prev)


def project_kernel(ctx_ref, *refs, shifts):
    count = 2 * len(shifts)
    pieces, o_ref, held, sem = refs[:count], refs[count], refs[count + 1], refs[count + 2]
    copies = [pltpu.make_async_copy(pieces[i], held.at[i], sem.at[i]) for i in range(count)]
    for copy in copies:
        copy.start()
    here = lax.axis_index("blk")
    core = lax.rem(here, 2)
    x, y = here // 8, lax.rem(here // 2, 4)
    ctx = jnp.concatenate([ctx_ref[i] for i in range(ctx_ref.shape[0])], axis=1)
    for i, (dx, dy) in enumerate(shifts):
        pair = 4 * lax.rem(x + dx, 2) + lax.rem(y + 4 - dy, 4)
        copies[2 * i].wait()
        copies[2 * i + 1].wait()
        w = jnp.concatenate([held[2 * i], held[2 * i + 1]], axis=1)
        out = jnp.dot(ctx, w, preferred_element_type=jnp.float32).astype(jnp.bfloat16)
        for part, where in ((0, core), (1, 1 - core)):
            at = pl.multiple_of((2 * pair + where) * LANES, LANES)
            o_ref[:, pl.ds(at, LANES)] = out[:, part * LANES : (part + 1) * LANES]


def project(ctx, pieces, shifts):
    _, rows, _ = ctx.shape
    depth = pieces[0].shape[0]
    width = len(pieces) * LANES
    return pl.pallas_call(
        functools.partial(project_kernel, shifts=shifts),
        out_shape=jax.ShapeDtypeStruct((rows, width), jnp.bfloat16),
        in_specs=[pl.BlockSpec(memory_space=pltpu.VMEM)]
        + [pl.BlockSpec(memory_space=pl.ANY)] * len(pieces),
        out_specs=pl.BlockSpec(memory_space=pltpu.VMEM),
        scratch_shapes=[
            pltpu.VMEM((len(pieces), depth, LANES), jnp.bfloat16),
            pltpu.SemaphoreType.DMA((len(pieces),)),
        ],
        compiler_params=pltpu.CompilerParams(vmem_limit_bytes=50 << 20),
        cost_estimate=pl.CostEstimate(
            flops=2 * rows * depth * width, bytes_accessed=2 * depth * width, transcendentals=0
        ),
        name="project",
    )(ctx, *pieces)


def layer(queries, key_rows, value_rows, w_out, first_key):
    place = lax.axis_index("blk")
    blks = lax.axis_size("blk")
    heads = lax.axis_size("head")
    rows = queries.shape[0]
    span = heads * rows
    split = lambda x: x.reshape(rows, heads, LANES).transpose(1, 0, 2)

    column = lax.dynamic_slice(w_out, (0, place * LANES), (w_out.shape[0], LANES))
    kvw = lax.all_to_all(
        jnp.stack(
            [
                split(key_rows),
                split(value_rows),
                jnp.broadcast_to(column[None], (heads,) + column.shape),
            ],
            axis=1,
        ),
        "head",
        0,
        0,
        tiled=True,
    )
    prev = lax.ppermute(kvw[:, :2], "blk", [(i, i + 1) for i in range(blks - 1)])
    query = split(queries)
    query = lax.all_to_all(query, "head", 0, 0, tiled=True)

    def shift(x, dx, dy):
        pairs = []
        for i in range(blks):
            x0, y0, core = i // 8, (i // 2) % 4, i % 2
            pairs.append((i, (x0 ^ dx) * 8 + ((y0 + dy) % 4) * 2 + core))
        return lax.ppermute(x, "blk", pairs)

    found = {(0, 0): kvw[:, 2].reshape(heads * w_out.shape[0], LANES)}
    for dx, dy in ((0, 1), (1, 3), (1, 1), (0, 3), (1, 0)):
        found[dx, dy] = shift(found[0, 0], dx, dy)
    for dx, dy in ((0, 1), (1, 3)):
        found[dx, 2] = shift(found[dx, dy], 0, dy)
    shifts = [(dx, dy) for dy in (0, 1, 3, 2) for dx in (0, 1)]
    pieces = []
    for at in shifts:
        other = lax.ppermute(found[at], "blk", [(i, i ^ 1) for i in range(blks)])
        pieces += [found[at], other]

    tile_start = (jnp.arange(span, dtype=jnp.int32) // TILE) * TILE
    low = first_key - (place * span - span) - tile_start
    low = jnp.broadcast_to(low[:, None], (span, LANES))
    ctx = attention(low, query, kvw, prev)
    ctx = lax.all_to_all(ctx, "head", 0, 0, tiled=True)
    return project(ctx, pieces, shifts)


def solution(mesh):
    placed = (
        P(("blk", "head"), None),
        P(("blk", "head"), None),
        P(("blk", "head"), None),
        P("head", None),
        P("blk"),
    )
    return jax.shard_map(
        layer, mesh=mesh, in_specs=placed, out_specs=P(("blk", "head"), None), check_vma=False
    )
```
